256 devices in a mesh: shard: 64 (over x, y_hi, z), tensor: 4 (over y_lo, core).
Axes of the slice: x: 4, y: 4 (y_hi: 2, y_lo: 2; y = y_hi * 2 + y_lo), z: 8, core: 2. Of those that a mesh axis runs over, the one named last changes fastest.
Arguments:
- gradient: bfloat16 [768, 3072], P('shard', 'tensor'), may hold values from -0.47851562 to 0.47851562
- moment: float32 [768, 3072], P('shard', 'tensor'), may hold values from -0.48 to 0.48
- second_moment: float32 [768, 3072], P('shard', 'tensor'), may hold values from 0.0001 to 0.01
- stat_left: float32 [768, 768], P('shard', 'tensor'), as said below
- stat_right: float32 [3072, 3072], P('shard', 'tensor'), as said below
- basis_left: float32 [768, 768], P('shard', 'tensor'), as said below
- basis_right: float32 [3072, 3072], P('shard', 'tensor'), as said below
Outputs:
- update: float32 [768, 3072], P('shard', 'tensor')
- moment_new: float32 [768, 3072], P('shard', 'tensor')
- second_new: float32 [768, 3072], P('shard', 'tensor')
- stat_left_new: float32 [768, 768], P('shard', 'tensor')
- stat_right_new: float32 [3072, 3072], P('shard', 'tensor')
- basis_left_new: float32 [768, 768], P('shard', 'tensor')
- basis_right_new: float32 [3072, 3072], P('shard', 'tensor')
The draws below stay inside these ranges and needn't reach their ends.
Inputs may be any that keep to these rules, and one draw needn't show every extreme that they name: `stat_left`: a symmetric matrix. `stat_right`: a symmetric matrix. `basis_left`: a square matrix of full rank. `basis_right`: a square matrix of full rank.
All inputs are finite; a program needn't handle non-finite values.
Results may differ from the reference program's by a relative error of at most 0.0018.
The reference program's roundings to bfloat16 on the way count: a program that leaves them out, or rounds other values in their place, can miss the bound.
Values may be sent and summed in bfloat16 or wider, within the bound.
No kernel may reach another device: no remote copies, remote signals or barrier semaphores. Data moves between devices by JAX's collectives and lax.ppermute only.
A program may use at most 64 MiB of HBM per device.

```python
import math
import jax
import jax.numpy as jnp

D = 768
FF = 3072
NS_ITERS = 2


def noise_matrix(key, order):
    return jax.random.normal(key, (order, order), jnp.float32)


def symmetric_stat(key, order, peak):
    key_rank, key_noise = jax.random.split(key)
    ranking = jax.random.permutation(key_rank, order).astype(jnp.float32) + 1.0
    level = peak * jnp.power(ranking, -0.75)
    noise_draw = noise_matrix(key_noise, order)
    off_diagonal = (noise_draw + noise_draw.T) * (0.4 / math.sqrt(2.0 * order))
    scaling = jnp.sqrt(level)
    return scaling[:, None] * scaling[None, :] * (jnp.eye(order, dtype=jnp.float32) + off_diagonal)


def near_identity(key, order):
    noise_draw = noise_matrix(key, order)
    return jnp.eye(order, dtype=jnp.float32) + noise_draw * (0.5 / math.sqrt(order))


def draw_stat_left(key, part):
    return symmetric_stat(jax.random.fold_in(key, 11), D, 40.0)


def draw_stat_right(key, part):
    return symmetric_stat(jax.random.fold_in(key, 23), FF, 10.0)


def draw_basis_left(key, part):
    return near_identity(jax.random.fold_in(key, 37), D)


def draw_basis_right(key, part):
    return near_identity(jax.random.fold_in(key, 41), FF)


def levels(stream_key, shape, cuts, low, high):
    level, own = 1.0, jax.random.fold_in(stream_key, 6)
    for position, parts in cuts:
        heights = jnp.exp(jax.random.uniform(jax.random.fold_in(own, position), (parts,), jnp.float32, low / len(cuts), high / len(cuts)))
        level = level * jnp.repeat(heights, shape[position] // parts).reshape([-1 if axis == position else 1 for axis in range(len(shape))])
    return level


def bell_draw(key, shape, scale, limit, cuts=(), held_as=jnp.bfloat16):
    loudness = levels(key, shape, cuts, -0.22, 0.18) if cuts else 1.0
    entries = jax.random.normal(key, shape, jnp.float32) * scale * loudness
    return jnp.minimum(jnp.maximum(entries, -limit), limit).astype(held_as)


def setup_inputs(seed: int = 0) -> dict:
    key_list = jax.random.split(jax.random.key(seed), 8)
    return {
        "gradient": bell_draw(key_list[0], (D, FF), 0.08, 0.47851562, ((0, 64), (1, 4))),
        "moment": bell_draw(key_list[1], (D, FF), 0.08, 0.48, ((0, 64), (1, 4)), jnp.float32),
        "second_moment": jnp.clip(jnp.exp(math.log(0.01) - 4.6051702 * jax.random.uniform(key_list[2], (D, FF), jnp.float32) ** levels(key_list[2], (D, FF), ((0, 64), (1, 4)), -0.2, 0.2)), 0.0001, 0.01),
        "stat_left": draw_stat_left(jax.random.fold_in(key_list[7], 71), 0),
        "stat_right": draw_stat_right(jax.random.fold_in(key_list[7], 71), 0),
        "basis_left": draw_basis_left(jax.random.fold_in(key_list[7], 71), 0),
        "basis_right": draw_basis_right(jax.random.fold_in(key_list[7], 71), 0),
    }


def orthogonalize(statistic, basis):
    power = jnp.dot(statistic.astype(jnp.bfloat16), basis.astype(jnp.bfloat16), preferred_element_type=jnp.float32)
    iterate = power / jnp.sqrt(jnp.sum(power * power) + 1e-06)
    for iteration in range(NS_ITERS):
        iterate_half = iterate.astype(jnp.bfloat16)
        gram_half = jnp.dot(iterate_half, iterate_half.T, preferred_element_type=jnp.float32).astype(jnp.bfloat16)
        iterate = 1.5 * iterate - 0.5 * jnp.dot(gram_half, iterate_half, preferred_element_type=jnp.float32)
    return iterate

def reference(gradient, moment, second_moment, stat_left, stat_right, basis_left, basis_right):
    stat_left_new = 0.95 * stat_left + 0.05 * jnp.dot(gradient, gradient.T, preferred_element_type=jnp.float32)
    stat_right_new = 0.95 * stat_right + 0.05 * jnp.dot(gradient.T, gradient, preferred_element_type=jnp.float32)
    basis_left_new = orthogonalize(stat_left_new, basis_left)
    basis_right_new = orthogonalize(stat_right_new, basis_right)
    moment_new = 0.9 * moment + 0.1 * gradient.astype(jnp.float32)
    moment_half = moment_new.astype(jnp.bfloat16)
    left_half = basis_left.astype(jnp.bfloat16)
    right_half = basis_right.astype(jnp.bfloat16)
    grad_right = jnp.dot(gradient, right_half, preferred_element_type=jnp.float32).astype(jnp.bfloat16)
    moment_right = jnp.dot(moment_half, right_half, preferred_element_type=jnp.float32).astype(jnp.bfloat16)
    grad_turned = jnp.dot(left_half.T, grad_right, preferred_element_type=jnp.float32)
    moment_turned = jnp.dot(left_half.T, moment_right, preferred_element_type=jnp.float32)
    second_new = 0.95 * second_moment + 0.05 * grad_turned * grad_turned
    scaled = (moment_turned / (jnp.sqrt(second_new) + 1e-08)).astype(jnp.bfloat16)
    back_half = jnp.dot(scaled, right_half.T, preferred_element_type=jnp.float32).astype(jnp.bfloat16)
    update = jnp.dot(left_half, back_half, preferred_element_type=jnp.float32)
    return (update, moment_new, second_new, stat_left_new, stat_right_new, basis_left_new, basis_right_new)
```

```python
import jax
import jax.numpy as jnp
from jax import lax
from jax.sharding import Mesh, PartitionSpec as P

BF = jnp.bfloat16
F32 = jnp.float32

AXES = ("x", "yh", "zq", "zp", "yl", "c")
SIZES = (4, 2, 4, 2, 2, 2)
SIZE = dict(zip(AXES, SIZES))
DEPTH = ("zq", "zp")
PLANE = ("x", "yh")
TENSOR = ("yl", "c")
ROWS = ("x", "yh", "zp")
COLS = ("yl", "zq")


def group(axes):
    total = 1
    for axis in axes:
        total *= SIZE[axis]
    return total


def exchange(pieces, axes):
    return lax.all_to_all(pieces, axes, 0, 0, tiled=True)


def gather(array, axes):
    return exchange(jnp.broadcast_to(array[None], (group(axes),) + array.shape), axes)


def swap_core(array):
    return lax.ppermute(array, "c", ((0, 1), (1, 0)))


def in_order(core, own, other):
    return jnp.stack([jnp.where(core == 0, own, other), jnp.where(core == 0, other, own)])


def grid_permute(array, flip):
    pairs = []
    for high in range(2):
        for low in range(2):
            for core in range(2):
                pairs.append(((high * 2 + low) * 2 + core, (core * 2 + (low ^ flip)) * 2 + high))
    return lax.ppermute(array, ("zq", "c"), pairs)


def to_grid(array, low):
    width = array.shape[1] // 2
    left, right = array[:, :width], array[:, width:]
    same = grid_permute(jnp.where(low == 0, left, right), 0)
    other = grid_permute(jnp.where(low == 0, right, left), 1)
    return in_order(low, same, other)


def to_natural(array, low):
    same = grid_permute(jnp.where(low == 0, array[0], array[1]), 0)
    other = grid_permute(jnp.where(low == 0, array[1], array[0]), 1)
    return jnp.concatenate(
        [jnp.where(low == 0, same, other), jnp.where(low == 0, other, same)], axis=1
    )


def dot(first, second, dims):
    return lax.dot_general(first, second, (dims, ((), ())), preferred_element_type=F32)


def contract_blocks(blocks, panel):
    return dot(blocks, panel, ((0, 2), (0, 1)))


def natural_rows(gathered):
    _, _, _, rows, width = gathered.shape
    parts = gathered.reshape(2, 4, 2, 2, 2, rows, width)
    return parts.transpose(1, 2, 0, 4, 3, 5, 6).reshape(8, 8 * rows, width)


def per_device(gradient, moment, second_moment, stat_left, stat_right, basis_left, basis_right):
    place = {axis: lax.axis_index(axis) for axis in AXES}
    core = place["c"]
    low = place["zq"] % 2
    depth = place["zq"] * 2 + place["zp"]
    shard = place["x"] * 16 + place["yh"] * 8 + depth
    tensor = place["yl"] * 2 + core
    rows, width = gradient.shape
    rows_right = stat_right.shape[0]
    width_left = stat_left.shape[1]
    order = 64 * rows
    half = width // 2

    moment_new = 0.9 * moment + 0.1 * gradient.astype(F32)
    moment_half = moment_new.astype(BF)
    left_half = basis_left.astype(BF)
    right_half = basis_right.astype(BF)

    grad_deep = gather(gradient, DEPTH).reshape(8 * rows, width)
    strips = jnp.stack(
        [
            lax.dynamic_slice_in_dim(grad_deep, half * side + rows_right * depth, rows_right, 1)
            for side in range(2)
        ]
    )
    strips = lax.ppermute(
        strips,
        ("x", "yl", "c"),
        [(first * 4 + second, second * 4 + first) for first in range(4) for second in range(4)],
    )
    strips = exchange(
        jnp.broadcast_to(strips[:, None], (2, 4) + strips.shape[1:]).reshape(
            8, 8 * rows, rows_right
        ),
        ("yh",) + TENSOR,
    )
    strip = (
        strips.reshape(2, 4, 8 * rows, rows_right).transpose(1, 0, 2, 3).reshape(order, rows_right)
    )
    grad_panel = gather(grad_deep, PLANE).reshape(order, width)

    basis_grid = to_grid(right_half, low).reshape(2 * rows_right, half)
    basis_own = gather(basis_grid, ROWS)
    basis_other = swap_core(basis_own)
    basis_panel = natural_rows(
        in_order(core, basis_own, basis_other).reshape(2, 16, 2, rows_right, half)
    )

    cross_right = dot(strip, grad_panel, ((0,), (0,)))
    stat_right_new = 0.95 * stat_right + 0.05 * cross_right
    stat_grid = to_grid(stat_right_new.astype(BF), low).reshape(2 * rows_right, half)
    stat_rows = gather(stat_grid, COLS)
    power = contract_blocks(stat_rows, basis_panel)

    def gather_sum(value, axes):
        return jnp.sum(gather(jnp.full((8, 128), value, F32), axes)[:, 0, 0])

    square = gather_sum(gather_sum(jnp.sum(power * power), ROWS + ("c",)), COLS) + 1e-06
    iterate = power
    for iteration in range(2):
        block = iterate.astype(BF)
        own = gather(block, ROWS).reshape(16 * block.shape[0], half)
        other = swap_core(own)
        panel = jnp.concatenate([own, other]).reshape(8, half, half)
        parts = jnp.stack(
            [dot(block, panel[piece], ((1,), (1,))).astype(BF) for piece in range(8)]
        )
        gram = jnp.sum(exchange(parts, COLS).astype(F32), axis=0)
        if iteration == 0:
            gram = gram / square
        gram_rows = gather(gram.astype(BF), COLS)
        iterate = 1.5 * iterate - 0.5 * contract_blocks(gram_rows, panel)
        if iteration == 0:
            iterate = iterate / jnp.sqrt(square)
    basis_right_new = to_natural(iterate.reshape(2, rows_right, half), low)

    left_rows = gather(left_half, TENSOR).transpose(1, 0, 2).reshape(rows, order)
    left_deep = gather(left_rows, DEPTH).reshape(8 * rows, order)
    left = gather(left_deep, PLANE).reshape(order, order)
    cross_parts = dot(gradient, grad_panel, ((1,), (1,)))
    cross_parts = cross_parts.reshape(rows, 4, width_left).transpose(1, 0, 2)
    cross_left = jnp.sum(exchange(cross_parts, TENSOR), axis=0)
    stat_left_new = 0.95 * stat_left + 0.05 * cross_left
    stat_full = gather(stat_left_new.astype(BF), TENSOR).transpose(1, 0, 2).reshape(rows, order)
    stat_full = gather(stat_full, DEPTH).reshape(8 * rows, order)
    stat_full = gather(stat_full, PLANE).reshape(order, order)
    power_left = dot(stat_full, left, ((1,), (0,)))
    iterate_left = power_left / jnp.sqrt(jnp.sum(power_left * power_left) + 1e-06)
    half_left = iterate_left.astype(BF)
    gram_left = dot(half_left, half_left, ((1,), (1,))).astype(BF)
    iterate_left = 1.5 * iterate_left - 0.5 * dot(gram_left, half_left, ((1,), (0,)))
    half_left = iterate_left.astype(BF)
    own_left = lax.dynamic_slice_in_dim(half_left, shard * rows, rows, 0)
    gram_own = dot(own_left, half_left, ((1,), (1,))).astype(BF)
    columns_left = lax.dynamic_slice_in_dim(half_left, tensor * width_left, width_left, 1)
    block_left = lax.dynamic_slice(
        iterate_left, (shard * rows, tensor * width_left), (rows, width_left)
    )
    basis_left_new = 1.5 * block_left - 0.5 * dot(gram_own, columns_left, ((1,), (0,)))

    both = to_grid(jnp.concatenate([gradient, moment_half]), low)
    both_rows = gather(both.reshape(4 * rows, half), COLS)
    rotated = contract_blocks(both_rows, basis_panel).astype(BF)

    def gather_rows(array):
        own = gather(array, ROWS)
        both = in_order(core, own, swap_core(own))
        return natural_rows(both).reshape(order, array.shape[2])

    rotated = rotated.reshape(2, 2, rows, half).transpose(0, 2, 1, 3).reshape(2, rows, 2 * half)
    rotated = gather_rows(rotated)
    starts = [
        rows * (16 * place["x"] + 8 * place["yh"] + 2 * (2 * core + side) + place["zp"])
        for side in range(2)
    ]
    left_columns = jnp.concatenate(
        [lax.dynamic_slice_in_dim(left, start, rows, 1) for start in starts], axis=1
    )
    left_own = jnp.concatenate([lax.dynamic_slice_in_dim(left, start, rows, 0) for start in starts])
    turned = dot(left_columns, rotated, ((0,), (0,)))
    grad_turned, moment_turned = turned[:, :half], turned[:, half:]
    second_grid = to_grid(second_moment, low).reshape(2 * rows, half)
    second_new = 0.95 * second_grid + 0.05 * grad_turned * grad_turned
    scaled = (moment_turned / (jnp.sqrt(second_new) + 1e-08)).astype(BF)
    back = jnp.stack([dot(scaled, basis_panel[piece], ((1,), (1,))) for piece in range(8)])
    back = jnp.sum(exchange(back, COLS), axis=0).astype(BF)
    back = gather_rows(back.reshape(2, rows, half))
    update = dot(left_own, back, ((1,), (0,)))
    result = jnp.concatenate(
        [update.reshape(2, rows, half), second_new.reshape(2, rows, half)], axis=1
    )
    result = to_natural(result, low)
    return (
        result[:rows],
        moment_new,
        result[rows:],
        stat_left_new,
        stat_right_new,
        basis_left_new,
        basis_right_new,
    )


def solution(mesh):
    parts = Mesh(mesh.devices.reshape(SIZES), AXES)
    spec = P(("x", "yh", "zq", "zp"), TENSOR)
    return jax.shard_map(
        per_device,
        mesh=parts,
        in_specs=(spec,) * 7,
        out_specs=(spec,) * 7,
        check_vma=False,
    )
```

```python
import jax
import jax.numpy as jnp
from jax import lax
from jax.sharding import Mesh, PartitionSpec as P

BF = jnp.bfloat16
F32 = jnp.float32

AXES = ("x", "yh", "zq", "zp", "yl", "c")
SIZES = (4, 2, 4, 2, 2, 2)
SIZE = dict(zip(AXES, SIZES))
DEPTH = ("zq", "zp")
PLANE = ("x", "yh")
TENSOR = ("yl", "c")
ROWS = ("x", "yh", "zp")
COLS = ("yl", "zq")


def group(axes):
    total = 1
    for axis in axes:
        total *= SIZE[axis]
    return total


def exchange(pieces, axes):
    return lax.all_to_all(pieces, axes, 0, 0, tiled=True)


def tensor_gather(array, yl, core):
    array = in_order(core, array, swap(array, "c"))
    array = in_order(yl, array, swap(array, "yl"))
    return array.transpose(2, 0, 1, 3).reshape(array.shape[2], 4 * array.shape[3])


def gather(array, axes):
    return exchange(jnp.broadcast_to(array[None], (group(axes),) + array.shape), axes)


def swap(array, axis, bit=1):
    pairs = [(index, index ^ bit) for index in range(SIZE[axis])]
    return lax.ppermute(array, axis, pairs)


def swap_core(array):
    return swap(array, "c")


def halve(array, side, axis, bit=1):
    mine = jnp.where(side == 0, array[0], array[1])
    other = jnp.where(side == 0, array[1], array[0])
    return mine + swap(other, axis, bit)


def in_order(core, own, other):
    return jnp.stack([jnp.where(core == 0, own, other), jnp.where(core == 0, other, own)])


def grid_permute(array, flip):
    pairs = []
    for high in range(2):
        for low in range(2):
            for core in range(2):
                pairs.append(((high * 2 + low) * 2 + core, (core * 2 + (low ^ flip)) * 2 + high))
    return lax.ppermute(array, ("zq", "c"), pairs)


def to_grid(array, low):
    width = array.shape[1] // 2
    left, right = array[:, :width], array[:, width:]
    same = grid_permute(jnp.where(low == 0, left, right), 0)
    other = grid_permute(jnp.where(low == 0, right, left), 1)
    return in_order(low, same, other)


def to_natural(array, low):
    same = grid_permute(jnp.where(low == 0, array[0], array[1]), 0)
    other = grid_permute(jnp.where(low == 0, array[1], array[0]), 1)
    return jnp.concatenate(
        [jnp.where(low == 0, same, other), jnp.where(low == 0, other, same)], axis=1
    )


def dot(first, second, dims):
    return lax.dot_general(first, second, (dims, ((), ())), preferred_element_type=F32)


def contract_blocks(blocks, panel):
    return dot(blocks, panel, ((0, 2), (0, 1)))


def natural_rows(gathered):
    _, _, _, rows, width = gathered.shape
    parts = gathered.reshape(2, 4, 2, 2, 2, rows, width)
    return parts.transpose(1, 2, 0, 4, 3, 5, 6).reshape(8, 8 * rows, width)


def split_scalar(value, width):
    high = value.astype(BF)
    rest = value - high.astype(F32)
    middle = rest.astype(BF)
    low = (rest - middle.astype(F32)).astype(BF)
    row = lax.broadcasted_iota(jnp.int32, (16, width), 0)
    return jnp.where(row == 0, high, jnp.where(row == 1, middle, low))


def join_scalar(blocks):
    return jnp.sum(blocks[:, :3, 0].astype(F32))


def per_device(gradient, moment, second_moment, stat_left, stat_right, basis_left, basis_right):
    place = {axis: lax.axis_index(axis) for axis in AXES}
    core = place["c"]
    low = place["zq"] % 2
    depth = place["zq"] * 2 + place["zp"]
    shard = place["x"] * 16 + place["yh"] * 8 + depth
    tensor = place["yl"] * 2 + core
    rows, width = gradient.shape
    rows_right = stat_right.shape[0]
    width_left = stat_left.shape[1]
    order = 64 * rows
    half = width // 2

    moment_new = 0.9 * moment + 0.1 * gradient.astype(F32)
    moment_half = moment_new.astype(BF)
    left_half = basis_left.astype(BF)
    right_half = basis_right.astype(BF)

    deep = gather(jnp.concatenate([gradient, left_half], axis=1), DEPTH)
    deep = deep.reshape(8 * rows, width + width_left)
    panels = gather(deep, PLANE).reshape(order, width + width_left)
    grad_panel = panels[:, :width]
    left = tensor_gather(panels[:, width:], place["yl"], core)
    strips = jnp.stack(
        [
            lax.dynamic_slice_in_dim(deep, half * side + rows_right * depth, rows_right, 1)
            for side in range(2)
        ]
    )
    strips = lax.ppermute(
        strips,
        ("x", "yl", "c"),
        [(first * 4 + second, second * 4 + first) for first in range(4) for second in range(4)],
    )
    strips = in_order(
        place["yh"],
        jnp.where(place["yh"] == 0, strips[0], strips[1]),
        swap(jnp.where(place["yh"] == 0, strips[1], strips[0]), "yh"),
    )
    strips = in_order(core, strips, swap(strips, "c"))
    strips = in_order(place["yl"], strips, swap(strips, "yl"))
    strip = strips.reshape(order, rows_right)

    both = to_grid(jnp.concatenate([gradient, moment_half]), low).reshape(4 * rows, half)
    both = in_order(low, both, swap(both, "zq", 1))
    both = in_order(place["zq"] // 2, both, swap(both, "zq", 2))
    both = in_order(place["yl"], both, swap(both, "yl"))
    both_rows = both.reshape(8, 4 * rows, half)

    basis_own = gather(to_grid(right_half, low).reshape(2 * rows_right, half), ROWS)
    basis_panel = natural_rows(
        in_order(core, basis_own, swap_core(basis_own)).reshape(2, 16, 2, rows_right, half)
    )

    cross_right = dot(strip, grad_panel, ((0,), (0,)))
    stat_right_new = 0.95 * stat_right + 0.05 * cross_right
    stat_grid = to_grid(stat_right_new.astype(BF), low).reshape(2 * rows_right, half)
    stat_rows = gather(stat_grid, COLS)
    product = contract_blocks(jnp.concatenate([stat_rows, both_rows], axis=1), basis_panel)
    power = product[: 2 * rows_right]
    square = jnp.sum(power * power)

    block = power.astype(BF)
    count = block.shape[0]
    rotated = product[count:].astype(BF)
    own = gather(jnp.concatenate([block, rotated, split_scalar(square, half)]), ROWS)
    other = swap_core(own)
    square = join_scalar(own[:, count + 4 * rows :]) + join_scalar(other[:, count + 4 * rows :])
    rotated = in_order(core, own[:, count : count + 4 * rows], other[:, count : count + 4 * rows])
    rotated = rotated.reshape(2, 4, 2, 2, 2, 2, rows, half).transpose(1, 2, 0, 4, 3, 6, 5, 7)
    rotated = rotated.reshape(order, 2 * half)

    def gram_parts(block, panel):
        return jnp.stack(
            [dot(block, panel[piece], ((1,), (1,))).astype(BF) for piece in range(8)]
        )

    panel = jnp.concatenate([own[:, :count], other[:, :count]]).reshape(8, half, half)
    extra = jnp.broadcast_to(split_scalar(square, half)[None], (8, 16, half))
    parts = exchange(jnp.concatenate([gram_parts(block, panel), extra], axis=1), COLS)
    square = join_scalar(parts[:, count:]) + 1e-06
    gram = jnp.sum(parts[:, :count].astype(F32), axis=0) / square
    gram_rows = gather(gram.astype(BF), COLS)
    iterate = 1.5 * power - 0.5 * contract_blocks(gram_rows, panel)
    iterate = iterate / jnp.sqrt(square)

    starts = [
        rows * (16 * place["x"] + 8 * place["yh"] + 2 * (2 * core + side) + place["zp"])
        for side in range(2)
    ]
    left_columns = jnp.concatenate(
        [lax.dynamic_slice_in_dim(left, start, rows, 1) for start in starts], axis=1
    )
    left_own = jnp.concatenate([lax.dynamic_slice_in_dim(left, start, rows, 0) for start in starts])
    turned = dot(left_columns, rotated, ((0,), (0,)))
    grad_turned, moment_turned = turned[:, :half], turned[:, half:]
    second_grid = to_grid(second_moment, low).reshape(2 * rows, half)
    second_new = 0.95 * second_grid + 0.05 * grad_turned * grad_turned
    scaled = (moment_turned / (jnp.sqrt(second_new) + 1e-08)).astype(BF)
    back = jnp.stack([dot(scaled, basis_panel[piece], ((1,), (1,))) for piece in range(8)])
    back = back.reshape(2, 2, 2, 2 * rows, half)
    back = halve(back, place["yl"], "yl")
    back = halve(back, place["zq"] // 2, "zq", 2)
    back = halve(back, low, "zq", 1).astype(BF)

    block = iterate.astype(BF)
    own = gather(jnp.concatenate([block, back]), ROWS)
    other = swap_core(own)
    back = in_order(core, own[:, count:], other[:, count:]).reshape(2, 16, 2, rows, half)
    back = natural_rows(back).reshape(order, half)
    panel = jnp.concatenate([own[:, :count], other[:, :count]]).reshape(8, half, half)
    parts = exchange(gram_parts(block, panel), COLS)
    gram_rows = gather(jnp.sum(parts.astype(F32), axis=0).astype(BF), COLS)
    iterate = 1.5 * iterate - 0.5 * contract_blocks(gram_rows, panel)
    basis_right_new = to_natural(iterate.reshape(2, rows_right, half), low)

    cross_parts = dot(gradient, grad_panel, ((1,), (1,)))
    cross_parts = cross_parts.reshape(rows, 2, 2, width_left).transpose(1, 2, 0, 3)
    cross_left = halve(halve(cross_parts, place["yl"], "yl"), core, "c")
    stat_left_new = 0.95 * stat_left + 0.05 * cross_left
    stat_full = tensor_gather(stat_left_new.astype(BF), place["yl"], core)
    stat_full = in_order(place["zp"], stat_full, swap(stat_full, "zp"))
    stat_full = in_order(low, stat_full, swap(stat_full, "zq", 1))
    stat_full = in_order(place["zq"] // 2, stat_full, swap(stat_full, "zq", 2))
    stat_full = in_order(place["yh"], stat_full, swap(stat_full, "yh"))
    stat_full = in_order(place["x"] % 2, stat_full, swap(stat_full, "x", 1))
    stat_full = in_order(place["x"] // 2, stat_full, swap(stat_full, "x", 2))
    stat_full = stat_full.reshape(order, order)
    power_left = dot(stat_full, left, ((1,), (0,)))
    iterate_left = power_left / jnp.sqrt(jnp.sum(power_left * power_left) + 1e-06)
    half_left = iterate_left.astype(BF)
    gram_left = dot(half_left, half_left, ((1,), (1,))).astype(BF)
    iterate_left = 1.5 * iterate_left - 0.5 * dot(gram_left, half_left, ((1,), (0,)))
    half_left = iterate_left.astype(BF)
    own_left = lax.dynamic_slice_in_dim(half_left, shard * rows, rows, 0)
    gram_own = dot(own_left, half_left, ((1,), (1,))).astype(BF)
    columns_left = lax.dynamic_slice_in_dim(half_left, tensor * width_left, width_left, 1)
    block_left = lax.dynamic_slice(
        iterate_left, (shard * rows, tensor * width_left), (rows, width_left)
    )
    basis_left_new = 1.5 * block_left - 0.5 * dot(gram_own, columns_left, ((1,), (0,)))

    update = dot(left_own, back, ((1,), (0,)))
    result = jnp.concatenate(
        [update.reshape(2, rows, half), second_new.reshape(2, rows, half)], axis=1
    )
    result = to_natural(result, low)
    return (
        result[:rows],
        moment_new,
        result[rows:],
        stat_left_new,
        stat_right_new,
        basis_left_new,
        basis_right_new,
    )


def solution(mesh):
    parts = Mesh(mesh.devices.reshape(SIZES), AXES)
    spec = P(("x", "yh", "zq", "zp"), TENSOR)
    return jax.shard_map(
        per_device,
        mesh=parts,
        in_specs=(spec,) * 7,
        out_specs=(spec,) * 7,
        check_vma=False,
    )
```

```python
import jax
import jax.numpy as jnp
from jax import lax
from jax.sharding import Mesh, PartitionSpec as P

BF = jnp.bfloat16
F32 = jnp.float32

AXES = ("x", "yh", "zq", "zp", "yl", "c")
SIZES = (4, 2, 4, 2, 2, 2)
SIZE = dict(zip(AXES, SIZES))
DEPTH = ("zq", "zp")
PLANE = ("x", "yh")
TENSOR = ("yl", "c")
ROWS = ("x", "yh", "zp")
COLS = ("yl", "zq")


def group(axes):
    total = 1
    for axis in axes:
        total *= SIZE[axis]
    return total


def exchange(pieces, axes):
    return lax.all_to_all(pieces, axes, 0, 0, tiled=True)


def tensor_gather(array, yl, core):
    array = in_order(core, array, swap(array, "c"))
    array = in_order(yl, array, swap(array, "yl"))
    return array.transpose(2, 0, 1, 3).reshape(array.shape[2], 4 * array.shape[3])


def gather(array, axes):
    return exchange(jnp.broadcast_to(array[None], (group(axes),) + array.shape), axes)


def swap(array, axis, bit=1):
    pairs = [(index, index ^ bit) for index in range(SIZE[axis])]
    return lax.ppermute(array, axis, pairs)


def swap_core(array):
    return swap(array, "c")


def after(array, *others):
    return lax.optimization_barrier((array,) + others)[0]


def halve(array, side, axis, bit=1):
    mine = jnp.where(side == 0, array[0], array[1])
    other = jnp.where(side == 0, array[1], array[0])
    return mine + swap(other, axis, bit)


def in_order(core, own, other):
    return jnp.stack([jnp.where(core == 0, own, other), jnp.where(core == 0, other, own)])


def grid_permute(array, flip):
    pairs = []
    for high in range(2):
        for low in range(2):
            for core in range(2):
                pairs.append(((high * 2 + low) * 2 + core, (core * 2 + (low ^ flip)) * 2 + high))
    return lax.ppermute(array, ("zq", "c"), pairs)


def to_grid(array, low):
    width = array.shape[1] // 2
    left, right = array[:, :width], array[:, width:]
    same = grid_permute(jnp.where(low == 0, left, right), 0)
    other = grid_permute(jnp.where(low == 0, right, left), 1)
    return in_order(low, same, other)


def to_natural(array, low):
    same = grid_permute(jnp.where(low == 0, array[0], array[1]), 0)
    other = grid_permute(jnp.where(low == 0, array[1], array[0]), 1)
    return jnp.concatenate(
        [jnp.where(low == 0, same, other), jnp.where(low == 0, other, same)], axis=1
    )


def dot(first, second, dims):
    return lax.dot_general(first, second, (dims, ((), ())), preferred_element_type=F32)


def contract_blocks(blocks, panel):
    return dot(blocks, panel, ((0, 2), (0, 1)))


def natural_rows(gathered):
    _, _, _, rows, width = gathered.shape
    parts = gathered.reshape(2, 4, 2, 2, 2, rows, width)
    return parts.transpose(1, 2, 0, 4, 3, 5, 6).reshape(8, 8 * rows, width)


def split_scalar(value, width):
    high = value.astype(BF)
    rest = value - high.astype(F32)
    middle = rest.astype(BF)
    low = (rest - middle.astype(F32)).astype(BF)
    row = lax.broadcasted_iota(jnp.int32, (16, width), 0)
    return jnp.where(row == 0, high, jnp.where(row == 1, middle, low))


def join_scalar(blocks):
    return jnp.sum(blocks[:, :3, 0].astype(F32))


def per_device(gradient, moment, second_moment, stat_left, stat_right, basis_left, basis_right):
    place = {axis: lax.axis_index(axis) for axis in AXES}
    core = place["c"]
    low = place["zq"] % 2
    depth = place["zq"] * 2 + place["zp"]
    shard = place["x"] * 16 + place["yh"] * 8 + depth
    tensor = place["yl"] * 2 + core
    rows, width = gradient.shape
    rows_right = stat_right.shape[0]
    width_left = stat_left.shape[1]
    order = 64 * rows
    half = width // 2

    moment_new = 0.9 * moment + 0.1 * gradient.astype(F32)
    moment_half = moment_new.astype(BF)
    left_half = basis_left.astype(BF)
    right_half = basis_right.astype(BF)

    deep = gather(jnp.concatenate([gradient, left_half], axis=1), DEPTH)
    deep = deep.reshape(8 * rows, width + width_left)
    panels = gather(deep, PLANE).reshape(order, width + width_left)
    grad_panel = panels[:, :width]

    floats = after(jnp.concatenate([stat_right, second_moment]), deep)
    halves = after(jnp.concatenate([right_half, gradient, moment_half]), deep)
    halves = to_grid(halves, low)
    floats = to_grid(floats, low)
    stat_grid = floats[:, :rows_right].reshape(2 * rows_right, half)
    second_grid = floats[:, rows_right:].reshape(2 * rows, half)
    basis_grid = halves[:, :rows_right].reshape(2 * rows_right, half)
    both = halves[:, rows_right:].reshape(4 * rows, half)

    basis_own = gather(after(basis_grid, panels), ROWS)

    part = jnp.where(low == 0, grad_panel[:, :half], grad_panel[:, half:])
    block_columns = jnp.where(core == place["zq"] // 2, part, swap_core(part))

    def strip_of(side):
        start = half * place["yh"] + rows_right * place["zp"] + 4 * rows_right * side
        return jnp.concatenate(
            [
                lax.dynamic_slice_in_dim(grad_panel, start + 2 * rows_right * b, rows_right, 1)
                for b in range(2)
            ],
            axis=1,
        )

    strip = jnp.where(core == place["x"] % 2, strip_of(core), swap_core(strip_of(1 - core)))
    strip = jnp.where(place["yl"] == place["x"] // 2, strip, swap(strip, "yl"))
    both = in_order(low, both, swap(after(both, panels), "zq", 1))
    both = in_order(place["zq"] // 2, both, swap(both, "zq", 2))
    cross_parts = dot(gradient, grad_panel, ((1,), (1,)))
    cross_parts = cross_parts.reshape(rows, 2, 2, width_left).transpose(1, 2, 0, 3)
    cross_left = halve(halve(cross_parts, place["yl"], "yl"), core, "c")
    stat_left_new = 0.95 * stat_left + 0.05 * cross_left
    left = in_order(core, panels[:, width:], swap_core(panels[:, width:]))

    stat_new = 0.95 * stat_grid + 0.05 * dot(strip, block_columns, ((0,), (0,)))
    stat_rows = gather(after(stat_new.astype(BF), basis_own, both, stat_left_new), COLS)

    basis_panel = natural_rows(
        in_order(core, basis_own, swap_core(basis_own)).reshape(2, 16, 2, rows_right, half)
    )
    both = in_order(place["yl"], both, swap(after(both, basis_own), "yl"))
    both_rows = both.reshape(8, 4 * rows, half)
    left = in_order(place["yl"], left, swap(after(left, basis_own), "yl"))
    left = left.transpose(2, 0, 1, 3).reshape(order, order)
    stat_full = tensor_gather(after(stat_left_new.astype(BF), basis_own), place["yl"], core)

    product = contract_blocks(jnp.concatenate([stat_rows, both_rows], axis=1), basis_panel)
    power = product[: 2 * rows_right]
    square = jnp.sum(power * power)

    block = power.astype(BF)
    count = block.shape[0]
    rotated = product[count:].astype(BF)
    block = after(block, stat_full)
    own = gather(jnp.concatenate([block, rotated, split_scalar(square, half)]), ROWS)

    stat_natural = to_natural(after(stat_new, stat_rows).reshape(2, rows_right, half), low)
    stat_full = after(stat_full, stat_rows)
    stat_full = in_order(place["zp"], stat_full, swap(stat_full, "zp"))
    stat_full = in_order(low, stat_full, swap(stat_full, "zq", 1))

    other = swap_core(own)
    square = join_scalar(own[:, count + 4 * rows :]) + join_scalar(other[:, count + 4 * rows :])
    rotated = in_order(core, own[:, count : count + 4 * rows], other[:, count : count + 4 * rows])
    rotated = rotated.reshape(2, 4, 2, 2, 2, 2, rows, half).transpose(1, 2, 0, 4, 3, 6, 5, 7)
    rotated = rotated.reshape(order, 2 * half)

    def gram_parts(block, panel):
        return [dot(block, panel[piece], ((1,), (1,))).astype(BF) for piece in range(4)]

    own_panel = own[:, :count].reshape(4, half, half)
    other_panel = other[:, :count].reshape(4, half, half)
    extra = jnp.broadcast_to(split_scalar(square, half)[None], (8, 16, half))
    parts = jnp.stack(gram_parts(block, own_panel) + gram_parts(block, other_panel))
    parts = after(jnp.concatenate([parts, extra], axis=1), stat_full, stat_natural)
    parts = exchange(parts, COLS)

    starts = [
        rows * (16 * place["x"] + 8 * place["yh"] + 2 * (2 * core + side) + place["zp"])
        for side in range(2)
    ]
    left_columns = jnp.concatenate(
        [lax.dynamic_slice_in_dim(left, start, rows, 1) for start in starts], axis=1
    )
    left_own = jnp.concatenate([lax.dynamic_slice_in_dim(left, start, rows, 0) for start in starts])
    turned = dot(left_columns, rotated, ((0,), (0,)))
    grad_turned, moment_turned = turned[:, :half], turned[:, half:]
    second_new = 0.95 * second_grid + 0.05 * grad_turned * grad_turned
    scaled = (moment_turned / (jnp.sqrt(second_new) + 1e-08)).astype(BF)
    back = jnp.stack([dot(scaled, basis_panel[piece], ((1,), (1,))) for piece in range(8)])
    back = back.reshape(2, 2, 2, 2 * rows, half)
    back = halve(back, place["yl"], "yl")
    stat_full = after(stat_full, own)
    stat_full = in_order(place["zq"] // 2, stat_full, swap(stat_full, "zq", 2))
    stat_full = in_order(place["yh"], stat_full, swap(stat_full, "yh"))

    square = join_scalar(parts[:, count:]) + 1e-06
    gram = jnp.sum(parts[:, :count].astype(F32), axis=0) / square
    gram_rows = gather(after(gram.astype(BF), stat_full, back), COLS)

    back = halve(after(back, parts), place["zq"] // 2, "zq", 2)
    back = halve(back, low, "zq", 1).astype(BF)
    stat_full = after(stat_full, parts)
    stat_full = in_order(place["x"] % 2, stat_full, swap(stat_full, "x", 1))

    def apply(gram_rows, own_panel, other_panel):
        first = contract_blocks(gram_rows[:4], own_panel)
        return first + contract_blocks(gram_rows[4:], other_panel)

    iterate = 1.5 * power - 0.5 * apply(gram_rows, own_panel, other_panel)
    iterate = iterate / jnp.sqrt(square)

    block = after(iterate.astype(BF), stat_full)
    own = gather(jnp.concatenate([block, back]), ROWS)
    stat_full = after(stat_full, gram_rows)
    stat_full = in_order(place["x"] // 2, stat_full, swap(stat_full, "x", 2))
    stat_full = stat_full.reshape(order, order)
    other = swap_core(own)
    back = in_order(core, own[:, count:], other[:, count:]).reshape(2, 16, 2, rows, half)
    back = natural_rows(back).reshape(order, half)
    own_panel = own[:, :count].reshape(4, half, half)
    other_panel = other[:, :count].reshape(4, half, half)
    parts = jnp.stack(gram_parts(block, own_panel) + gram_parts(block, other_panel))
    parts = exchange(after(parts, stat_full), COLS)
    gram_rows = gather(jnp.sum(parts.astype(F32), axis=0).astype(BF), COLS)
    iterate = 1.5 * iterate - 0.5 * apply(gram_rows, own_panel, other_panel)
    basis_right_new = to_natural(iterate.reshape(2, rows_right, half), low)

    power_left = dot(stat_full, left, ((1,), (0,)))
    iterate_left = power_left / jnp.sqrt(jnp.sum(power_left * power_left) + 1e-06)
    half_left = iterate_left.astype(BF)
    gram_left = dot(half_left, half_left, ((1,), (1,))).astype(BF)
    iterate_left = 1.5 * iterate_left - 0.5 * dot(gram_left, half_left, ((1,), (0,)))
    half_left = iterate_left.astype(BF)
    own_left = lax.dynamic_slice_in_dim(half_left, shard * rows, rows, 0)
    gram_own = dot(own_left, half_left, ((1,), (1,))).astype(BF)
    columns_left = lax.dynamic_slice_in_dim(half_left, tensor * width_left, width_left, 1)
    block_left = lax.dynamic_slice(
        iterate_left, (shard * rows, tensor * width_left), (rows, width_left)
    )
    basis_left_new = 1.5 * block_left - 0.5 * dot(gram_own, columns_left, ((1,), (0,)))

    update = dot(left_own, back, ((1,), (0,)))
    result = jnp.concatenate(
        [update.reshape(2, rows, half), second_new.reshape(2, rows, half)], axis=1
    )
    result = to_natural(result, low)
    return (
        result[:rows],
        moment_new,
        result[rows:],
        stat_left_new,
        stat_natural,
        basis_left_new,
        basis_right_new,
    )


def solution(mesh):
    parts = Mesh(mesh.devices.reshape(SIZES), AXES)
    spec = P(("x", "yh", "zq", "zp"), TENSOR)
    return jax.shard_map(
        per_device,
        mesh=parts,
        in_specs=(spec,) * 7,
        out_specs=(spec,) * 7,
        check_vma=False,
    )
```

```python
import jax
import jax.numpy as jnp
from jax import lax
from jax.sharding import Mesh, PartitionSpec as P

BF = jnp.bfloat16
F32 = jnp.float32

AXES = ("x", "yh", "zq", "zp", "yl", "c")
SIZES = (4, 2, 4, 2, 2, 2)
SIZE = dict(zip(AXES, SIZES))
DEPTH = ("zq", "zp")
PLANE = ("x", "yh")
TENSOR = ("yl", "c")
ROWS = ("x", "yh", "zp")
COLS = ("yl", "zq")


def group(axes):
    total = 1
    for axis in axes:
        total *= SIZE[axis]
    return total


def exchange(pieces, axes):
    return lax.all_to_all(pieces, axes, 0, 0, tiled=True)


def tensor_gather(array, yl, core):
    array = in_order(core, array, swap(array, "c"))
    array = in_order(yl, array, swap(array, "yl"))
    return array.transpose(2, 0, 1, 3).reshape(array.shape[2], 4 * array.shape[3])


def spread(array, axes):
    return jnp.broadcast_to(array[None], (group(axes),) + array.shape)


def gather(array, axes):
    return exchange(spread(array, axes), axes)


def swap(array, axis, bit=1):
    pairs = [(index, index ^ bit) for index in range(SIZE[axis])]
    return lax.ppermute(array, axis, pairs)


def swap_core(array):
    return swap(array, "c")


def after(array, *others):
    return lax.optimization_barrier((array,) + others)[0]


def halve(array, side, axis, bit=1):
    mine = jnp.where(side == 0, array[0], array[1])
    other = jnp.where(side == 0, array[1], array[0])
    return mine + swap(other, axis, bit)


def in_order(core, own, other):
    return jnp.stack([jnp.where(core == 0, own, other), jnp.where(core == 0, other, own)])


def grid_permute(array, flip):
    pairs = []
    for high in range(2):
        for low in range(2):
            for core in range(2):
                pairs.append(((high * 2 + low) * 2 + core, (core * 2 + (low ^ flip)) * 2 + high))
    return lax.ppermute(array, ("zq", "c"), pairs)


def to_grid(array, low):
    width = array.shape[1] // 2
    left, right = array[:, :width], array[:, width:]
    same = grid_permute(jnp.where(low == 0, left, right), 0)
    other = grid_permute(jnp.where(low == 0, right, left), 1)
    return in_order(low, same, other)


def to_natural(array, low):
    same = grid_permute(jnp.where(low == 0, array[0], array[1]), 0)
    other = grid_permute(jnp.where(low == 0, array[1], array[0]), 1)
    return jnp.concatenate(
        [jnp.where(low == 0, same, other), jnp.where(low == 0, other, same)], axis=1
    )


def dot(first, second, dims):
    return lax.dot_general(first, second, (dims, ((), ())), preferred_element_type=F32)


def contract_blocks(blocks, panel):
    return dot(blocks, panel, ((0, 2), (0, 1)))


def natural_rows(gathered):
    _, _, _, rows, width = gathered.shape
    parts = gathered.reshape(2, 4, 2, 2, 2, rows, width)
    return parts.transpose(1, 2, 0, 4, 3, 5, 6).reshape(8, 8 * rows, width)


def split_scalar(value, width):
    high = value.astype(BF)
    rest = value - high.astype(F32)
    middle = rest.astype(BF)
    low = (rest - middle.astype(F32)).astype(BF)
    row = lax.broadcasted_iota(jnp.int32, (16, width), 0)
    return jnp.where(row == 0, high, jnp.where(row == 1, middle, low))


def join_scalar(blocks):
    return jnp.sum(blocks[:, :3, 0].astype(F32))


def per_device(gradient, moment, second_moment, stat_left, stat_right, basis_left, basis_right):
    place = {axis: lax.axis_index(axis) for axis in AXES}
    core = place["c"]
    low = place["zq"] % 2
    depth = place["zq"] * 2 + place["zp"]
    shard = place["x"] * 16 + place["yh"] * 8 + depth
    tensor = place["yl"] * 2 + core
    rows, width = gradient.shape
    rows_right = stat_right.shape[0]
    width_left = stat_left.shape[1]
    order = 64 * rows
    half = width // 2

    moment_new = 0.9 * moment + 0.1 * gradient.astype(F32)
    moment_half = moment_new.astype(BF)
    left_half = basis_left.astype(BF)
    right_half = basis_right.astype(BF)

    payload = jnp.concatenate([gradient, left_half], axis=1)
    deep = gather(payload, DEPTH).reshape(8 * rows, width + width_left)
    padded = jnp.pad(left_half, ((0, 0), (0, width - width_left)))
    halves = jnp.concatenate([right_half, gradient, moment_half, padded])
    halves = to_grid(after(halves, payload), low)
    basis_grid = halves[:, :rows_right].reshape(2 * rows_right, half)
    both = halves[:, rows_right:].reshape(6 * rows, half)

    panels = gather(deep, PLANE).reshape(order, width + width_left)
    floats = to_grid(after(jnp.concatenate([stat_right, second_moment]), deep), low)
    stat_grid = floats[:, :rows_right].reshape(2 * rows_right, half)
    second_grid = floats[:, rows_right:].reshape(2 * rows, half)
    both = in_order(low, both, swap(after(both, deep), "zq", 1))
    both = in_order(place["zq"] // 2, both, swap(both, "zq", 2))
    grad_panel, left_panel = panels[:, :width], panels[:, width:]

    basis_own = gather(after(basis_grid, panels, both, floats), ROWS)
    part = jnp.where(low == 0, grad_panel[:, :half], grad_panel[:, half:])

    def strip_of(side):
        start = half * place["yh"] + rows_right * (place["zp"] + 4 * side)
        fine = 8 * rows * place["yh"] + rows * (place["zp"] + 4 * side)
        pieces = [
            lax.dynamic_slice_in_dim(grad_panel, start + 2 * rows_right * b, rows_right, 1)
            for b in range(2)
        ] + [
            lax.dynamic_slice_in_dim(left_panel, fine + 2 * rows * b, rows, 1) for b in range(2)
        ]
        return jnp.concatenate(pieces, axis=1)

    strip = jnp.where(core == place["x"] % 2, strip_of(core), swap_core(strip_of(1 - core)))
    block_columns = jnp.where(core == place["zq"] // 2, part, swap_core(part))
    cross_parts = dot(after(gradient, strip), grad_panel, ((1,), (1,)))
    strip = jnp.where(place["yl"] == place["x"] // 2, strip, swap(strip, "yl"))
    left_columns = strip[:, 2 * rows_right :]
    strip = strip[:, : 2 * rows_right]
    cross_parts = cross_parts.reshape(rows, 2, 2, width_left).transpose(1, 2, 0, 3)
    cross_left = halve(halve(cross_parts, place["yl"], "yl"), core, "c")
    stat_left_new = 0.95 * stat_left + 0.05 * cross_left

    stat_new = 0.95 * stat_grid + 0.05 * dot(strip, block_columns, ((0,), (0,)))
    payload = after(stat_new.astype(BF), basis_own)
    payload = spread(payload, COLS)
    stat_rows = exchange(payload, COLS)
    basis_other = swap_core(basis_own)
    basis_panel = natural_rows(
        in_order(core, after(basis_own, payload), basis_other).reshape(2, 16, 2, rows_right, half)
    )
    both = in_order(place["yl"], both, swap(after(both, payload), "yl"))
    both_rows = both.reshape(8, 6 * rows, half)
    left_own = both.reshape(2, 2, 2, 2, 3, rows, half)[:, :, 0, :, 2, :, :width_left]
    left_own = left_own.transpose(2, 3, 0, 1, 4).reshape(2 * rows, order)
    left_rows = tensor_gather(after(stat_left_new.astype(BF), payload), place["yl"], core)
    power_left = dot(left_rows, left_panel, ((1,), (0,)))
    square_left = jnp.sum(power_left * power_left)
    left_full = jnp.concatenate(
        [power_left.astype(BF), split_scalar(square_left, width_left)[: 16 - rows]]
    )

    product = contract_blocks(jnp.concatenate([stat_rows, both_rows], axis=1), basis_panel)
    count = 2 * rows_right
    power = product[:count]
    square = jnp.sum(power * power)
    block = power.astype(BF)
    rotated = product[count:].reshape(2, 3 * rows, half)[:, : 2 * rows].astype(BF)
    payload = jnp.concatenate(
        [block, rotated.reshape(4 * rows, half), split_scalar(square, half)]
    )
    payload = after(payload, left_full)
    payload = spread(payload, ROWS)
    own = exchange(payload, ROWS)
    left_full = after(left_full, payload)
    left_full = in_order(place["yl"], left_full, swap(left_full, "yl"))
    left_full = in_order(place["zp"], left_full, swap(left_full, "zp"))
    other = swap_core(own)

    def gram_parts(block, panel):
        return [dot(block, panel[piece], ((1,), (1,))).astype(BF) for piece in range(4)]

    def apply(gram_rows, own_panel, other_panel):
        first = contract_blocks(gram_rows[:4], own_panel)
        return first + contract_blocks(gram_rows[4:], other_panel)

    own_panel = own[:, :count].reshape(4, half, half)
    other_panel = other[:, :count].reshape(4, half, half)
    square = join_scalar(own[:, count + 4 * rows :]) + join_scalar(other[:, count + 4 * rows :])
    extra = jnp.broadcast_to(split_scalar(square, half)[None], (8, 16, half))
    payload = jnp.stack(gram_parts(block, own_panel) + gram_parts(block, other_panel))
    payload = after(jnp.concatenate([payload, extra], axis=1), left_full)
    parts = exchange(payload, COLS)
    left_full = after(left_full, payload)
    left_full = in_order(low, left_full, swap(left_full, "zq", 1))
    left_full = in_order(place["zq"] // 2, left_full, swap(left_full, "zq", 2))
    rotated = in_order(
        core,
        after(own[:, count : count + 4 * rows], payload),
        after(other[:, count : count + 4 * rows], payload),
    )
    rotated = rotated.reshape(2, 4, 2, 2, 2, 2, rows, half).transpose(1, 2, 0, 4, 3, 6, 5, 7)
    rotated = rotated.reshape(order, 2 * half)
    turned = dot(left_columns, rotated, ((0,), (0,)))
    grad_turned, moment_turned = turned[:, :half], turned[:, half:]
    second_new = 0.95 * second_grid + 0.05 * grad_turned * grad_turned
    scaled = (moment_turned / (jnp.sqrt(second_new) + 1e-08)).astype(BF)
    back = jnp.stack([dot(scaled, basis_panel[piece], ((1,), (1,))) for piece in range(8)])
    back = back.reshape(2, 2, 2, 2 * rows, half)
    back = halve(back, place["yl"], "yl")

    square = join_scalar(parts[:, count:]) + 1e-06
    gram = jnp.sum(parts[:, :count].astype(F32), axis=0) / square
    payload = after(gram.astype(BF), left_full, back)
    payload = spread(payload, COLS)
    gram_rows = exchange(payload, COLS)
    back = halve(after(back, payload), place["zq"] // 2, "zq", 2)
    back = halve(back, low, "zq", 1).astype(BF)
    left_full = after(left_full, payload)
    left_full = in_order(place["yh"], left_full, swap(left_full, "yh"))
    left_full = in_order(place["x"] % 2, left_full, swap(left_full, "x", 1))

    iterate = 1.5 * power - 0.5 * apply(gram_rows, own_panel, other_panel)
    iterate = iterate / jnp.sqrt(square)
    block = iterate.astype(BF)
    payload = after(jnp.concatenate([block, back]), left_full)
    payload = spread(payload, ROWS)
    own = exchange(payload, ROWS)
    left_full = after(left_full, payload)
    left_full = in_order(place["x"] // 2, left_full, swap(left_full, "x", 2))
    left_full = left_full.reshape(64, 2, 16, width_left)
    left_full = in_order(core, left_full, swap_core(left_full))
    stat_natural = to_natural(after(stat_new, payload).reshape(2, rows_right, half), low)
    other = swap_core(own)

    own_panel = own[:, :count].reshape(4, half, half)
    other_panel = other[:, :count].reshape(4, half, half)
    payload = jnp.stack(gram_parts(block, own_panel) + gram_parts(block, other_panel))
    payload = after(payload, left_full, stat_natural)
    parts = exchange(payload, COLS)
    back = in_order(core, after(own[:, count:], payload), after(other[:, count:], payload))
    back = natural_rows(back.reshape(2, 16, 2, rows, half)).reshape(order, half)
    update = dot(left_own, back, ((1,), (0,)))
    result = jnp.concatenate(
        [update.reshape(2, rows, half), second_new.reshape(2, rows, half)], axis=1
    )
    left_full = after(left_full, payload)
    square_left = jnp.sum(left_full[:, :, :, rows : rows + 3, 0].astype(F32)) + 1e-06
    left_full = left_full[:, :, :, :rows].transpose(1, 3, 2, 0, 4).reshape(order, order)

    payload = jnp.sum(parts.astype(F32), axis=0).astype(BF)
    payload = spread(payload, COLS)
    gram_rows = exchange(payload, COLS)
    result = to_natural(after(result, payload), low)
    norm_left = jnp.sqrt(square_left)
    gram_left = (dot(left_full, left_full, ((1,), (1,))) / square_left).astype(BF)
    next_left = 1.5 * left_full.astype(F32) - 0.5 * dot(gram_left, left_full, ((1,), (0,)))
    next_left = (next_left / norm_left).astype(BF)

    def own_rows(array):
        return lax.dynamic_slice_in_dim(array, shard * rows, rows, 0)

    def own_columns(array):
        return lax.dynamic_slice_in_dim(array, tensor * width_left, width_left, 1)

    block_left = 1.5 * power_left - 0.5 * dot(
        own_rows(gram_left), own_columns(left_full), ((1,), (0,))
    )
    gram_own = dot(own_rows(next_left), next_left, ((1,), (1,))).astype(BF)
    basis_left_new = 1.5 * (block_left / norm_left) - 0.5 * dot(
        gram_own, own_columns(next_left), ((1,), (0,))
    )
    iterate = 1.5 * iterate - 0.5 * apply(gram_rows, own_panel, other_panel)
    basis_right_new = to_natural(iterate.reshape(2, rows_right, half), low)
    return (
        result[:rows],
        moment_new,
        result[rows:],
        stat_left_new,
        stat_natural,
        basis_left_new,
        basis_right_new,
    )


def solution(mesh):
    parts = Mesh(mesh.devices.reshape(SIZES), AXES)
    spec = P(("x", "yh", "zq", "zp"), TENSOR)
    return jax.shard_map(
        per_device,
        mesh=parts,
        in_specs=(spec,) * 7,
        out_specs=(spec,) * 7,
        check_vma=False,
    )
```

```python
import jax
import jax.numpy as jnp
from jax import lax
from jax.sharding import Mesh, PartitionSpec as P

BF = jnp.bfloat16
F32 = jnp.float32

AXES = ("x", "yh", "zq", "zp", "yl", "c")
SIZES = (4, 2, 4, 2, 2, 2)
SIZE = dict(zip(AXES, SIZES))
DEPTH = ("zq", "zp")
PLANE = ("x", "yh")
TENSOR = ("yl", "c")
ROWS = ("x", "yh", "zp")
COLS = ("yl", "zq")


def group(axes):
    total = 1
    for axis in axes:
        total *= SIZE[axis]
    return total


def exchange(pieces, axes):
    return lax.all_to_all(pieces, axes, 0, 0, tiled=True)


def tensor_gather(array, yl, core):
    array = in_order(core, array, swap(array, "c"))
    array = in_order(yl, array, swap(array, "yl"))
    return array.transpose(2, 0, 1, 3).reshape(array.shape[2], 4 * array.shape[3])


def spread(array, axes):
    return jnp.broadcast_to(array[None], (group(axes),) + array.shape)


def gather(array, axes):
    return exchange(spread(array, axes), axes)


def swap(array, axis, bit=1):
    pairs = [(index, index ^ bit) for index in range(SIZE[axis])]
    return lax.ppermute(array, axis, pairs)


def swap_core(array):
    return swap(array, "c")


def after(array, *others):
    return lax.optimization_barrier((array,) + others)[0]


def halve(array, side, axis, bit=1):
    mine = jnp.where(side == 0, array[0], array[1])
    other = jnp.where(side == 0, array[1], array[0])
    return mine + swap(other, axis, bit)


def in_order(core, own, other):
    return jnp.stack([jnp.where(core == 0, own, other), jnp.where(core == 0, other, own)])


def grid_permute(array, flip):
    pairs = []
    for high in range(2):
        for low in range(2):
            for core in range(2):
                pairs.append(((high * 2 + low) * 2 + core, (core * 2 + (low ^ flip)) * 2 + high))
    return lax.ppermute(array, ("zq", "c"), pairs)


def to_grid(array, low):
    width = array.shape[1] // 2
    left, right = array[:, :width], array[:, width:]
    same = grid_permute(jnp.where(low == 0, left, right), 0)
    other = grid_permute(jnp.where(low == 0, right, left), 1)
    return in_order(low, same, other)


def to_natural(array, low):
    same = grid_permute(jnp.where(low == 0, array[0], array[1]), 0)
    other = grid_permute(jnp.where(low == 0, array[1], array[0]), 1)
    return jnp.concatenate(
        [jnp.where(low == 0, same, other), jnp.where(low == 0, other, same)], axis=1
    )


def dot(first, second, dims):
    return lax.dot_general(first, second, (dims, ((), ())), preferred_element_type=F32)


def contract_blocks(blocks, panel):
    return dot(blocks, panel, ((0, 2), (0, 1)))


def natural_rows(gathered):
    _, _, _, rows, width = gathered.shape
    parts = gathered.reshape(2, 4, 2, 2, 2, rows, width)
    return parts.transpose(1, 2, 0, 4, 3, 5, 6).reshape(8, 8 * rows, width)


def split_scalar(value, width):
    high = value.astype(BF)
    rest = value - high.astype(F32)
    middle = rest.astype(BF)
    low = (rest - middle.astype(F32)).astype(BF)
    row = lax.broadcasted_iota(jnp.int32, (8, width), 0)
    return jnp.where(row == 0, high, jnp.where(row == 1, middle, low))


def join_scalar(blocks):
    return jnp.sum(blocks[:, :3, 0].astype(F32))


def per_device(gradient, moment, second_moment, stat_left, stat_right, basis_left, basis_right):
    place = {axis: lax.axis_index(axis) for axis in AXES}
    core = place["c"]
    low = place["zq"] % 2
    depth = place["zq"] * 2 + place["zp"]
    shard = place["x"] * 16 + place["yh"] * 8 + depth
    tensor = place["yl"] * 2 + core
    rows, width = gradient.shape
    rows_right = stat_right.shape[0]
    width_left = stat_left.shape[1]
    order = 64 * rows
    half = width // 2

    moment_new = 0.9 * moment + 0.1 * gradient.astype(F32)
    moment_half = moment_new.astype(BF)
    left_half = basis_left.astype(BF)
    right_half = basis_right.astype(BF)

    payload = jnp.concatenate([gradient, left_half], axis=1)
    deep = gather(payload, DEPTH).reshape(8 * rows, width + width_left)
    padded = jnp.pad(left_half, ((0, 0), (0, width - width_left)))
    halves = jnp.concatenate([right_half, gradient, moment_half, padded])
    halves = to_grid(after(halves, payload), low)
    basis_grid = halves[:, :rows_right].reshape(2 * rows_right, half)
    both = halves[:, rows_right:].reshape(6 * rows, half)

    panels = gather(deep, PLANE).reshape(order, width + width_left)
    floats = to_grid(after(jnp.concatenate([stat_right, second_moment]), deep), low)
    stat_grid = floats[:, :rows_right].reshape(2 * rows_right, half)
    second_grid = floats[:, rows_right:].reshape(2 * rows, half)
    both = in_order(low, both, swap(after(both, deep), "zq", 1))
    both = in_order(place["zq"] // 2, both, swap(both, "zq", 2))
    grad_panel, left_panel = panels[:, :width], panels[:, width:]

    basis_own = gather(after(basis_grid, panels, both, floats), ROWS)
    part = jnp.where(low == 0, grad_panel[:, :half], grad_panel[:, half:])

    def strip_of(side):
        start = half * place["yh"] + rows_right * (place["zp"] + 4 * side)
        fine = 8 * rows * place["yh"] + rows * (place["zp"] + 4 * side)
        pieces = [
            lax.dynamic_slice_in_dim(grad_panel, start + 2 * rows_right * b, rows_right, 1)
            for b in range(2)
        ] + [
            lax.dynamic_slice_in_dim(left_panel, fine + 2 * rows * b, rows, 1) for b in range(2)
        ]
        return jnp.concatenate(pieces, axis=1)

    strip = jnp.where(core == place["x"] % 2, strip_of(core), swap_core(strip_of(1 - core)))
    block_columns = jnp.where(core == place["zq"] // 2, part, swap_core(part))
    cross_parts = dot(after(gradient, strip), grad_panel, ((1,), (1,)))
    strip = jnp.where(place["yl"] == place["x"] // 2, strip, swap(strip, "yl"))
    left_columns = strip[:, 2 * rows_right :]
    strip = strip[:, : 2 * rows_right]
    cross_parts = cross_parts.reshape(rows, 2, 2, width_left).transpose(1, 2, 0, 3)
    cross_left = halve(halve(cross_parts, place["yl"], "yl"), core, "c")
    stat_left_new = 0.95 * stat_left + 0.05 * cross_left

    stat_new = 0.95 * stat_grid + 0.05 * dot(strip, block_columns, ((0,), (0,)))
    payload = after(stat_new.astype(BF), basis_own)
    payload = spread(payload, COLS)
    stat_rows = exchange(payload, COLS)
    basis_other = swap_core(basis_own)
    basis_panel = natural_rows(
        in_order(core, after(basis_own, payload), basis_other).reshape(2, 16, 2, rows_right, half)
    )
    both = in_order(place["yl"], both, swap(after(both, payload), "yl"))
    both_rows = both.reshape(8, 6 * rows, half)
    left_own = both.reshape(2, 2, 2, 2, 3, rows, half)[:, :, 0, :, 2, :, :width_left]
    left_own = left_own.transpose(2, 3, 0, 1, 4).reshape(2 * rows, order)
    left_rows = tensor_gather(after(stat_left_new.astype(BF), payload), place["yl"], core)
    power_left = dot(left_rows, left_panel, ((1,), (0,)))
    square_left = jnp.sum(power_left * power_left)
    left_full = jnp.concatenate(
        [power_left.astype(BF), split_scalar(square_left, width_left)[: 16 - rows]]
    )

    product = contract_blocks(jnp.concatenate([stat_rows, both_rows], axis=1), basis_panel)
    count = 2 * rows_right
    power = product[:count]
    square = jnp.sum(power * power)
    block = power.astype(BF)
    rotated = product[count:].reshape(2, 3 * rows, half)[:, : 2 * rows].astype(BF)
    payload = jnp.concatenate(
        [block, rotated.reshape(4 * rows, half), split_scalar(square, half)]
    )
    payload = after(payload, left_full)
    payload = spread(payload, ROWS)
    own = exchange(payload, ROWS)
    left_full = after(left_full, payload)
    left_full = in_order(place["yl"], left_full, swap(left_full, "yl"))
    left_full = in_order(low, left_full, swap(left_full, "zq", 1))
    left_full = in_order(place["zq"] // 2, left_full, swap(left_full, "zq", 2))
    stat_natural = to_natural(after(stat_new, payload).reshape(2, rows_right, half), low)
    other = swap_core(own)

    def by_core(array):
        return (
            jnp.where(core == 0, array[0], array[1]),
            jnp.where(core == 0, array[1], array[0]),
        )

    turn = after(left_columns, payload).reshape(8, 2, 2, 2, rows, 2 * rows)
    turn = turn.transpose(1, 0, 3, 2, 4, 5).reshape(2, 16, 2, rows, 2 * rows)
    blank = jnp.zeros_like(turn)
    turn = jnp.stack(
        [
            jnp.concatenate([turn, blank], axis=4),
            jnp.concatenate([blank, turn], axis=4),
        ],
        axis=3,
    )
    turn = by_core(turn.reshape(2, order, 4 * rows))
    spin = after(left_own, payload).reshape(2 * rows, 8, 2, 2, 2, rows)
    spin = by_core(spin.transpose(2, 0, 1, 4, 3, 5).reshape(2, 2 * rows, order // 2))

    def gram_parts(block, panel):
        return [dot(block, panel[piece], ((1,), (1,))).astype(BF) for piece in range(4)]

    def apply(gram_rows, own_panel, other_panel):
        first = contract_blocks(gram_rows[:4], own_panel)
        return first + contract_blocks(gram_rows[4:], other_panel)

    own_panel = own[:, :count].reshape(4, half, half)
    other_panel = other[:, :count].reshape(4, half, half)
    square = join_scalar(own[:, count + 4 * rows :]) + join_scalar(other[:, count + 4 * rows :])
    extra = jnp.broadcast_to(split_scalar(square, half)[None], (8, 8, half))
    payload = jnp.stack(gram_parts(block, own_panel) + gram_parts(block, other_panel))
    payload = after(jnp.concatenate([payload, extra], axis=1), left_full, stat_natural)
    parts = exchange(payload, COLS)
    left_full = after(left_full, payload)
    left_full = in_order(place["zp"], left_full, swap(left_full, "zp"))
    left_full = in_order(place["x"] % 2, left_full, swap(left_full, "x", 1))

    def turn_rows(array, factor):
        array = after(array[:, count : count + 4 * rows], payload).reshape(order, half)
        return dot(factor, array, ((0,), (0,)))

    turned = turn_rows(own, turn[0]) + turn_rows(other, turn[1])
    grad_turned, moment_turned = turned[: 2 * rows], turned[2 * rows :]
    second_new = 0.95 * second_grid + 0.05 * grad_turned * grad_turned
    scaled = (moment_turned / (jnp.sqrt(second_new) + 1e-08)).astype(BF)
    back = jnp.stack([dot(scaled, basis_panel[piece], ((1,), (1,))) for piece in range(8)])
    back = back.reshape(2, 2, 2, 2 * rows, half)
    back = halve(back, place["yl"], "yl")

    square = join_scalar(parts[:, count:]) + 1e-06
    gram = jnp.sum(parts[:, :count].astype(F32), axis=0) / square
    payload = after(gram.astype(BF), left_full)
    payload = spread(payload, COLS)
    gram_rows = exchange(payload, COLS)
    back = halve(back, place["zq"] // 2, "zq", 2)
    back = halve(back, low, "zq", 1).astype(BF)
    left_full = after(left_full, payload)
    left_full = in_order(place["x"] // 2, left_full, swap(left_full, "x", 2))
    left_full = in_order(place["yh"], left_full, swap(left_full, "yh"))

    iterate = 1.5 * power - 0.5 * apply(gram_rows, own_panel, other_panel)
    iterate = iterate / jnp.sqrt(square)
    block = iterate.astype(BF)
    payload = after(jnp.concatenate([block, back]), left_full)
    payload = spread(payload, ROWS)
    own = exchange(payload, ROWS)
    left_full = after(left_full, payload)
    left_full = left_full.reshape(2, 4, 2, 4, 2, 16, width_left)
    left_full = in_order(core, left_full, swap_core(left_full))
    other = swap_core(own)

    own_panel = own[:, :count].reshape(4, half, half)
    other_panel = other[:, :count].reshape(4, half, half)
    payload = jnp.stack(gram_parts(block, own_panel) + gram_parts(block, other_panel))
    payload = after(payload, left_full)
    parts = exchange(payload, COLS)

    def spin_rows(array, factor):
        array = after(array[:, count:], payload).reshape(order // 2, half)
        return dot(factor, array, ((1,), (0,)))

    update = spin_rows(own, spin[0]) + spin_rows(other, spin[1])
    result = jnp.concatenate(
        [update.reshape(2, rows, half), second_new.reshape(2, rows, half)], axis=1
    )
    left_full = after(left_full, payload)
    square_left = jnp.sum(left_full[..., rows : rows + 3, 0].astype(F32)) + 1e-06
    left_full = left_full[..., :rows, :].transpose(2, 1, 4, 3, 6, 5, 0, 7).reshape(order, order)

    payload = jnp.sum(parts.astype(F32), axis=0).astype(BF)
    payload = spread(payload, COLS)
    gram_rows = exchange(payload, COLS)
    result = to_natural(after(result, payload), low)
    norm_left = jnp.sqrt(square_left)
    gram_left = (dot(left_full, left_full, ((1,), (1,))) / square_left).astype(BF)
    next_left = 1.5 * left_full.astype(F32) - 0.5 * dot(gram_left, left_full, ((1,), (0,)))
    next_left = (next_left / norm_left).astype(BF)

    def own_rows(array):
        return lax.dynamic_slice_in_dim(array, shard * rows, rows, 0)

    def own_columns(array):
        return lax.dynamic_slice_in_dim(array, tensor * width_left, width_left, 1)

    block_left = 1.5 * power_left - 0.5 * dot(
        own_rows(gram_left), own_columns(left_full), ((1,), (0,))
    )
    gram_own = dot(own_rows(next_left), next_left, ((1,), (1,))).astype(BF)
    basis_left_new = 1.5 * (block_left / norm_left) - 0.5 * dot(
        gram_own, own_columns(next_left), ((1,), (0,))
    )
    iterate = 1.5 * iterate - 0.5 * apply(gram_rows, own_panel, other_panel)
    basis_right_new = to_natural(iterate.reshape(2, rows_right, half), low)
    return (
        result[:rows],
        moment_new,
        result[rows:],
        stat_left_new,
        stat_natural,
        basis_left_new,
        basis_right_new,
    )


def solution(mesh):
    parts = Mesh(mesh.devices.reshape(SIZES), AXES)
    spec = P(("x", "yh", "zq", "zp"), TENSOR)
    return jax.shard_map(
        per_device,
        mesh=parts,
        in_specs=(spec,) * 7,
        out_specs=(spec,) * 7,
        check_vma=False,
    )
```
